512 devices in a mesh: view: 64 (over y, z), head: 8 (over x, core).
Axes of the slice: x: 4, y: 4, z: 16, core: 2. Of those that a mesh axis runs over, the one named last changes fastest.
Arguments:
- feats: bfloat16 [65536, 640], P(('view', 'head')), may hold values from -6 to 6
- norm_gain: float32 [640], replicated, may hold values from 0.1 to 1.9
- w_query: bfloat16 [640, 640], P('head'), may hold values from -1 to 1
- w_key: bfloat16 [640, 640], P('head'), may hold values from -0.25 to 0.25
- w_value: bfloat16 [640, 640], P('head'), may hold values from -0.25 to 0.25
- w_out: bfloat16 [640, 640], P('head'), may hold values from -1 to 1
- cond_feats: bfloat16 [3072, 640], P('view'), may hold values from -60 to 60
- cond_wk: bfloat16 [640, 640], P('head'), may hold values from -0.25 to 0.25
- cond_wv: bfloat16 [640, 640], P('head'), may hold values from -0.25 to 0.25
- neighbours: int32 [2, 64, 32], replicated, may hold values from 0 to 63, as said below
- counts: int32 [64], P('view'), may hold values from 1 to 32, as said below
Outputs:
- mixed: bfloat16 [65536, 640], P(('view', 'head'))
The draws below stay inside these ranges and needn't reach their ends.
Inputs may be any that keep to these rules, and one draw needn't show every extreme that they name: `neighbours`: A device holds one view; devices are numbered by their view index and their order closes into a loop. The lists of one device's views name views of the devices 1 to 4 places before and after it in that loop only, exactly 4 entries for each of these 8 devices. Entries 0 to counts[v] - 1 of view v's list are valid, the rest are padding; some view has all 32 valid.
All inputs are finite; a program needn't handle non-finite values.
Results may differ from the reference program's by a relative error of at most 0.02.
The reference program's roundings to bfloat16 on the way count: a program that leaves them out, or rounds other values in their place, can miss the bound.
Values may be sent and summed in bfloat16 or wider, within the bound.
No kernel may reach another device: no remote copies, remote signals or barrier semaphores. Data moves between devices by JAX's collectives and lax.ppermute only.
A program may use at most 64 MiB of HBM per device.

```python
import math
import jax
import jax.numpy as jnp
from jax import lax

D = 640
HEADS = 8
TOK = 1024
BLOCK = 128
NB = 32
RADIUS = 4
NCOND = 3
VD = 1
VIEWS = 64
CAP = 4
N_HEAD = 8


def draw_neighbours(key, part):
    devices = VIEWS // VD
    entries = VD * NB
    steps_out = jnp.arange(1, RADIUS + 1, dtype=jnp.int32)
    offsets = jnp.repeat(jnp.concatenate([steps_out, -steps_out]), CAP)
    subkeys = jax.random.split(jax.random.fold_in(key, 7), devices)

    def device_lists(subkey, device):
        second, third, fourth = jax.random.split(subkey, 3)
        places = jax.random.permutation(second, entries)
        owner = (device + offsets[places] + devices) % devices
        inner = jax.random.randint(third, (entries,), 0, VD)
        block = jax.random.randint(fourth, (entries,), 0, TOK // BLOCK)
        return (owner * VD + inner, block)
    source, block = jax.vmap(device_lists)(subkeys, jnp.arange(devices, dtype=jnp.int32))
    return jnp.stack([source.reshape(VIEWS, NB), block.reshape(VIEWS, NB)]).astype(jnp.int32)


def draw_counts(key, part):
    first, second = jax.random.split(jax.random.fold_in(key, 13))
    drawn = jax.random.randint(first, (VIEWS,), 1, NB + 1)
    fullest = jax.random.randint(second, (), 0, VIEWS)
    return jnp.where(jnp.arange(VIEWS) == fullest, NB, drawn).astype(jnp.int32)


def draw_cond_feats(key, part):
    first = jax.random.fold_in(jax.random.fold_in(key, 17), 0)
    total_rows = NCOND * TOK
    base = jax.random.normal(first, (total_rows, D), jnp.float32)
    return jnp.clip(base, -60.0, 60.0).astype(jnp.bfloat16)


def steps_of(own_key, shape, cuts, low, largest):
    def one(dim, shards_of):
        steps = jax.random.uniform(jax.random.fold_in(jax.random.fold_in(own_key, 6), dim), (shards_of,), jnp.float32, low / len(cuts), largest / len(cuts))
        return jnp.repeat(jnp.exp(steps), shape[dim] // shards_of).reshape((-1,) + (1,) * (len(shape) - dim - 1))

    factor_of = one(*cuts[0])
    for cut in cuts[1:]:
        factor_of = factor_of * one(*cut)
    return factor_of


def centred(rng, shape, scale, reach, cuts=(), kind=jnp.bfloat16):
    values = jax.random.normal(rng, shape, jnp.float32) * scale
    if len(cuts) > 0:
        values = steps_of(rng, shape, cuts, -0.22, 0.18) * values
    return jnp.clip(values, min=-reach, max=reach).astype(kind)


def setup_inputs(seed: int = 0) -> dict:
    seeds = jax.random.split(jax.random.key(seed), 12)
    return {
        "feats": centred(seeds[0], (VIEWS * TOK, D), 1.0, 6.0, ((0, 512),)),
        "norm_gain": jnp.clip(1.0 + 0.18 * jax.random.normal(seeds[1], (D,), jnp.float32), 0.1, 1.9),
        "w_query": centred(seeds[2], (D, D), (D // 16) ** -0.5, 1.0, ((0, 8),)),
        "w_key": centred(seeds[3], (D, D), D ** -0.5, 0.25, ((0, 8),)),
        "w_value": centred(seeds[4], (D, D), D ** -0.5, 0.25, ((0, 8),)),
        "w_out": centred(seeds[5], (D, D), (D // 16) ** -0.5, 1.0, ((0, 8),)),
        "cond_feats": draw_cond_feats(jax.random.fold_in(seeds[11], 71), 0),
        "cond_wk": centred(seeds[7], (D, D), D ** -0.5, 0.25, ((0, 8),)),
        "cond_wv": centred(seeds[8], (D, D), D ** -0.5, 0.25, ((0, 8),)),
        "neighbours": draw_neighbours(jax.random.fold_in(seeds[11], 71), 0),
        "counts": draw_counts(jax.random.fold_in(seeds[11], 71), 0),
    }


def project_rows(inputs, weight):
    return lax.dot_general(inputs, weight, (((1,), (1,)), ((), ())), preferred_element_type=jnp.float32)

def group_terms(query, keys, values, scale):
    scores = jnp.einsum('qhe,khe->hqk', query.astype(jnp.float32), keys.astype(jnp.float32)) * scale
    top = lax.optimization_barrier(jnp.max(scores, axis=-1))
    weights = jnp.exp(scores - top[..., None]).astype(jnp.bfloat16)
    total = lax.optimization_barrier(jnp.sum(weights.astype(jnp.float32), axis=-1))
    summed = jnp.einsum('hqk,khe->hqe', weights.astype(jnp.float32), values.astype(jnp.float32))
    return (top, total, summed)

def block_terms(query, keys, values, scale):
    scores = jnp.einsum('qhe,jkhe->hjqk', query.astype(jnp.float32), keys.astype(jnp.float32)) * scale
    top = lax.optimization_barrier(jnp.max(scores, axis=-1))
    weights = jnp.exp(scores - top[..., None]).astype(jnp.bfloat16)
    total = lax.optimization_barrier(jnp.sum(weights.astype(jnp.float32), axis=-1))
    summed = jnp.einsum('hjqk,jkhe->hjqe', weights.astype(jnp.float32), values.astype(jnp.float32))
    return (top, total, summed)

def start_state(own, far):
    own_top, own_total, own_sum = own
    far_top, far_total, far_sum = far
    peak = jnp.maximum(own_top, far_top)
    own_factor = jnp.exp(own_top - peak)
    far_factor = jnp.exp(far_top - peak)
    total = own_factor * own_total + far_factor * far_total
    summed = own_factor[..., None] * own_sum + far_factor[..., None] * far_sum
    return (peak, total, summed)

def absorb(state, tops, totals, sums, valid):
    peak, total, summed = state
    tops = jnp.where(valid[None, :, None], tops, -1e+30)
    new_peak = jnp.maximum(peak, lax.optimization_barrier(jnp.max(tops, axis=1)))
    old_factor = jnp.exp(peak - new_peak)
    factor = jnp.exp(tops - new_peak[:, None, :])
    total = old_factor * total + lax.optimization_barrier(jnp.sum(factor * totals, axis=1))
    summed = old_factor[..., None] * summed + lax.optimization_barrier(jnp.sum(factor[..., None] * sums, axis=1))
    return (new_peak, total, summed)

def reference(feats, norm_gain, w_query, w_key, w_value, w_out, cond_feats, cond_wk, cond_wv, neighbours, counts):
    rows = feats.astype(jnp.float32)
    center = lax.optimization_barrier(jnp.mean(rows, axis=-1, keepdims=True))
    spread = lax.optimization_barrier(jnp.mean(jnp.square(rows - center), axis=-1, keepdims=True))
    normed = ((rows - center) * lax.rsqrt(spread + 1e-05) * norm_gain).astype(jnp.bfloat16)
    query = project_rows(normed, w_query).astype(jnp.bfloat16)
    key = project_rows(normed, w_key).astype(jnp.bfloat16)
    value = project_rows(normed, w_value).astype(jnp.bfloat16)
    cond_key = project_rows(cond_feats, cond_wk).astype(jnp.bfloat16)
    cond_value = project_rows(cond_feats, cond_wv).astype(jnp.bfloat16)
    head_size = D // HEADS
    scale = 1.0 / math.sqrt(head_size)
    per_view = TOK // BLOCK
    key_tiles = key.reshape(VIEWS * per_view, BLOCK, HEADS, head_size)
    value_tiles = value.reshape(VIEWS * per_view, BLOCK, HEADS, head_size)
    far_keys = cond_key.reshape(NCOND * TOK, HEADS, head_size)
    far_values = cond_value.reshape(NCOND * TOK, HEADS, head_size)
    rows_block = min(256, TOK)

    def one_view(view_index):
        start = view_index * TOK
        query_view = lax.dynamic_slice_in_dim(query, start, TOK, 0).reshape(TOK // rows_block, rows_block, HEADS, head_size)
        keys_view = lax.dynamic_slice_in_dim(key, start, TOK, 0).reshape(TOK, HEADS, head_size)
        values_view = lax.dynamic_slice_in_dim(value, start, TOK, 0).reshape(TOK, HEADS, head_size)
        tile_rows = (neighbours[0, view_index] * per_view + neighbours[1, view_index]).astype(jnp.int32)
        near_keys = key_tiles[tile_rows]
        near_values = value_tiles[tile_rows]
        valid = jnp.arange(NB, dtype=jnp.int32) < counts[view_index]

        def one_block(query_part):
            state = start_state(group_terms(query_part, keys_view, values_view, scale), group_terms(query_part, far_keys, far_values, scale))
            tops, totals, sums = block_terms(query_part, near_keys, near_values, scale)
            peak, total, summed = absorb(state, tops, totals, sums, valid)
            return summed / total[..., None]
        outcome = lax.map(one_block, query_view)
        return jnp.transpose(outcome, (0, 2, 1, 3)).reshape(TOK, HEADS * head_size)
    attended = lax.map(one_view, jnp.arange(VIEWS, dtype=jnp.int32))
    attended = attended.reshape(VIEWS * TOK, D).astype(jnp.bfloat16)
    group_width = HEADS // N_HEAD * head_size
    mixed = jnp.zeros((VIEWS * TOK, D), jnp.float32)
    for group in range(N_HEAD):
        lower = group * group_width
        partial_g = jnp.dot(attended[:, lower:lower + group_width], w_out[lower:lower + group_width], preferred_element_type=jnp.float32).astype(jnp.bfloat16)
        partial_g = lax.optimization_barrier(partial_g)
        mixed = mixed + partial_g.astype(jnp.float32)
    return mixed.astype(jnp.bfloat16)
```

```python
import math

import jax
import jax.numpy as jnp
from jax import lax
from jax.experimental import pallas as pl
from jax.experimental.pallas import tpu as pltpu
from jax.sharding import PartitionSpec as P

D = 640
HEADS = 8
TOK = 1024
BLOCK = 128
NB = 32
RADIUS = 4
HS = D // HEADS
PER_VIEW = TOK // BLOCK
YS, ZS, XS = 4, 16, 4
CAP = NB // (2 * RADIUS)
KPAD = 128
VPAD = 96
QT = 256
CHUNK = 512
COEF = math.log2(math.e) / math.sqrt(HS)
BF = jnp.bfloat16
F32 = jnp.float32


Z_GROUPS = [[y * ZS + z for z in range(ZS)] for y in range(YS)]
Y_GROUPS = [[y * ZS + z for y in range(YS)] for z in range(ZS)]
X_GROUPS = [[2 * x + c for x in range(XS)] for c in range(2)]


def nt(a, b):
    return lax.dot_general(a, b, (((1,), (1,)), ((), ())), preferred_element_type=F32)


def gather_by_all_to_all(piece, axis, groups, n):
    copies = jnp.broadcast_to(piece[None], (n,) + piece.shape)
    return lax.all_to_all(copies, axis, 0, 0, axis_index_groups=groups, tiled=True)


def shifted(x, distance):
    n = lax.axis_size("view")
    return lax.ppermute(x, "view", [(i, (i + distance) % n) for i in range(n)])


def params(mib=None):
    return pltpu.CompilerParams(vmem_limit_bytes=(mib or 32) << 20)


def vmem_specs(n):
    return [pl.BlockSpec(memory_space=pltpu.VMEM)] * n


SMEM = pl.BlockSpec(memory_space=pltpu.SMEM)


def qkv_kernel(core_ref, w_ref, mine_ref, other_ref, q_ref, kv_ref):
    core = core_ref[0]
    for which, rows in ((0, mine_ref), (1, other_ref)):
        parity = core if which == 0 else 1 - core
        out = nt(w_ref[...], rows[...]).astype(BF)
        for x in range(XS):
            part = out[:, x * BLOCK : (x + 1) * BLOCK]
            off = pl.multiple_of((2 * x + parity) * BLOCK, BLOCK)
            q_ref[:, pl.ds(off, BLOCK)] = part[:HS]
            kv_ref[:, pl.ds(off, BLOCK)] = part[HS:]


def project(core, w_qkv, mine, other):
    return pl.pallas_call(
        qkv_kernel,
        out_shape=(
            jax.ShapeDtypeStruct((HS, TOK), BF),
            jax.ShapeDtypeStruct((2 * HS, TOK), BF),
        ),
        in_specs=[SMEM] + vmem_specs(3),
        out_specs=tuple(vmem_specs(2)),
        compiler_params=params(),
        name="qkv",
    )(core, w_qkv, mine, other)


def fill_query(q_ref, qs):
    qs[:HS, :] = q_ref[...]
    rows = lax.broadcasted_iota(jnp.int32, (KPAD - HS, TOK), 0)
    qs[HS:, :] = jnp.where(rows == 0, 1.0, 0.0).astype(BF)


def fill_ones(vs, keys):
    rows = lax.broadcasted_iota(jnp.int32, (VPAD - HS, keys), 0)
    vs[HS:, :] = jnp.where(rows == 0, 1.0, 0.0).astype(BF)


def turned(kt, bias):
    rows = lax.broadcasted_iota(jnp.int32, (KPAD - HS, kt.shape[1]), 0)
    extra = jnp.where(rows == 0, bias, 0.0).astype(BF)
    return jnp.concatenate([kt, extra], axis=0).T


def absorb(qs, keys_of, vs, n_keys, state, store):
    def tile(i, _):
        off = pl.multiple_of(i * QT, QT)
        q = qs[:, pl.ds(off, QT)]
        peak, acc = state(off)
        for c in range(n_keys // CHUNK):
            s = jnp.dot(keys_of(c), q, preferred_element_type=F32)
            top = jnp.max(s, axis=0, keepdims=True)
            if peak is not None:
                top = jnp.maximum(peak, top)
            p = jnp.exp2((s - top) * COEF).astype(BF)
            add = jnp.dot(vs[:, c * CHUNK : (c + 1) * CHUNK], p, preferred_element_type=F32)
            if peak is None:
                acc = add
            else:
                acc = acc * jnp.exp2((peak - top) * COEF) + add
            peak = top
        store(off, i, peak, acc)
        return 0

    lax.fori_loop(0, TOK // QT, tile, 0)


def own_kernel(q_ref, kv_ref, m_ref, a_ref, qs, ks, vs):
    fill_query(q_ref, qs)
    fill_ones(vs, TOK)
    vs[:HS, :] = kv_ref[HS:, :]
    for b in range(TOK // CHUNK):
        ks[b * CHUNK : (b + 1) * CHUNK, :] = turned(kv_ref[:HS, b * CHUNK : (b + 1) * CHUNK], 0.0)

    def store(off, i, peak, acc):
        m_ref[:, pl.ds(off, QT)] = peak
        a_ref[:, pl.ds(off, QT)] = acc

    absorb(qs, lambda c: ks[c * CHUNK : (c + 1) * CHUNK, :], vs, TOK, lambda off: (None, None), store)


STATE = (
    jax.ShapeDtypeStruct((1, TOK), F32),
    jax.ShapeDtypeStruct((VPAD, TOK), F32),
)


def attend_own(q, kv):
    return pl.pallas_call(
        own_kernel,
        out_shape=STATE,
        in_specs=vmem_specs(2),
        out_specs=tuple(vmem_specs(2)),
        scratch_shapes=[
            pltpu.VMEM((KPAD, TOK), BF),
            pltpu.VMEM((TOK, KPAD), BF),
            pltpu.VMEM((VPAD, TOK), BF),
        ],
        compiler_params=params(),
        cost_estimate=pl.CostEstimate(flops=400_000_000, bytes_accessed=1_000_000, transcendentals=1 << 20),
        name="own",
    )(q, kv)


def cond_kernel(q_ref, k_ref, vt_ref, m_in, a_in, m_ref, a_ref, qs, vs):
    fill_query(q_ref, qs)
    qs[HS:, :] = jnp.zeros((KPAD - HS, TOK), BF)
    n = vt_ref.shape[1]
    fill_ones(vs, n)
    vs[:HS, :] = vt_ref[...]

    def store(off, i, peak, acc):
        m_ref[:, pl.ds(off, QT)] = peak
        a_ref[:, pl.ds(off, QT)] = acc

    absorb(
        qs,
        lambda c: k_ref[c * CHUNK : (c + 1) * CHUNK, :],
        vs,
        n,
        lambda off: (m_in[:, pl.ds(off, QT)], a_in[:, pl.ds(off, QT)]),
        store,
    )


def attend_cond(q, k, vt, state):
    n = vt.shape[1]
    return pl.pallas_call(
        cond_kernel,
        out_shape=STATE,
        in_specs=vmem_specs(5),
        out_specs=tuple(vmem_specs(2)),
        scratch_shapes=[pltpu.VMEM((KPAD, TOK), BF), pltpu.VMEM((VPAD, n), BF)],
        compiler_params=params(),
        cost_estimate=pl.CostEstimate(flops=1_200_000_000, bytes_accessed=3_000_000, transcendentals=3 << 20),
        name="cond",
    )(q, k, vt, *state)


def near_kernel(distance, last, sc, q_ref, kvp_ref, kvm_ref, m_in, a_in, *rest):
    outs, (qs, ks, vs, blocks, valid) = rest[:-5], rest[-5:]
    n = 2 * CAP * BLOCK
    me, limit = sc[2 * NB], sc[2 * NB + 1]
    peers = sc[2 * NB + 2]
    before = lax.rem(me - distance + peers, peers)
    after = lax.rem(me + distance, peers)

    def look(j, counts):
        lo, hi = counts
        s, b = sc[j], sc[NB + j]
        is_lo, is_hi = s == before, s == after
        slot = jnp.where(is_lo, lo, jnp.where(is_hi, hi, 2 * CAP))
        blocks[slot] = b
        valid[slot] = (j < limit).astype(jnp.int32)
        return lo + is_lo.astype(jnp.int32), hi + is_hi.astype(jnp.int32)

    lax.fori_loop(0, NB, look, (jnp.int32(0), jnp.int32(CAP)))
    fill_query(q_ref, qs)
    fill_ones(vs, n)
    for i in range(2 * CAP):
        kv = kvp_ref if i < CAP else kvm_ref
        off = pl.multiple_of(blocks[i] * BLOCK, BLOCK)
        bias = jnp.where(valid[i] > 0, 0.0, -1e30).astype(F32)
        ks[i * BLOCK : (i + 1) * BLOCK, :] = turned(kv[:HS, pl.ds(off, BLOCK)], bias)
        vs[:HS, i * BLOCK : (i + 1) * BLOCK] = kv[HS:, pl.ds(off, BLOCK)]

    def store(off, i, peak, acc):
        if last:
            done = (acc[:HS] / acc[HS : HS + 1]).astype(BF)
            for t in range(QT // BLOCK):
                outs[0][i * (QT // BLOCK) + t] = done[:, t * BLOCK : (t + 1) * BLOCK]
        else:
            outs[0][:, pl.ds(off, QT)] = peak
            outs[1][:, pl.ds(off, QT)] = acc

    absorb(
        qs,
        lambda c: ks[c * CHUNK : (c + 1) * CHUNK, :],
        vs,
        n,
        lambda off: (m_in[:, pl.ds(off, QT)], a_in[:, pl.ds(off, QT)]),
        store,
    )


def attend_near(distance, last, scalars, q, kvp, kvm, state):
    n = 2 * CAP * BLOCK

    def kernel(*refs):
        near_kernel(distance, last, *refs)

    return pl.pallas_call(
        kernel,
        out_shape=jax.ShapeDtypeStruct((PER_VIEW, HS, BLOCK), BF) if last else STATE,
        in_specs=[SMEM] + vmem_specs(5),
        out_specs=vmem_specs(1)[0] if last else tuple(vmem_specs(2)),
        scratch_shapes=[
            pltpu.VMEM((KPAD, TOK), BF),
            pltpu.VMEM((n, KPAD), BF),
            pltpu.VMEM((VPAD, n), BF),
            pltpu.SMEM((16,), jnp.int32),
            pltpu.SMEM((16,), jnp.int32),
        ],
        compiler_params=params(),
        cost_estimate=pl.CostEstimate(flops=400_000_000, bytes_accessed=2_000_000, transcendentals=1 << 20),
        name=f"near{distance}",
    )(scalars, q, kvp, kvm, *state)


def out_kernel(a_ref, w_ref, o_ref):
    total = None
    for g in range(HEADS):
        part = lax.dot_general(a_ref[g], w_ref[g], (((0,), (0,)), ((), ())), preferred_element_type=F32)
        part = part.astype(BF).astype(F32)
        total = part if total is None else total + part
    o_ref[...] = total.astype(BF)


def project_out(attended, w_out):
    return pl.pallas_call(
        out_kernel,
        out_shape=jax.ShapeDtypeStruct((BLOCK, D), BF),
        in_specs=vmem_specs(2),
        out_specs=vmem_specs(1)[0],
        compiler_params=params(),
        name="out",
    )(attended, w_out)


def per_device(
    feats,
    norm_gain,
    w_query,
    w_key,
    w_value,
    w_out,
    cond_feats,
    cond_wk,
    cond_wv,
    neighbours,
    counts,
):
    view = lax.axis_index("view")
    head = lax.axis_index("head")
    peers = lax.axis_size("view")
    cond_w = jnp.concatenate([cond_wk, cond_wv], axis=0)
    cond_piece = nt(cond_feats, cond_w).astype(BF).reshape(-1, 128)
    rows = feats.astype(F32)
    center = jnp.mean(rows, axis=-1, keepdims=True)
    spread = jnp.mean(jnp.square(rows - center), axis=-1, keepdims=True)
    normed = ((rows - center) * lax.rsqrt(spread + 1e-05) * norm_gain).astype(BF)
    mine = gather_by_all_to_all(normed, "head", X_GROUPS, XS).reshape(XS * BLOCK, D)
    other = lax.ppermute(mine, "head", [(h, h ^ 1) for h in range(HEADS)])
    cond_z = gather_by_all_to_all(cond_piece, "view", Z_GROUPS, ZS)
    cond_all = gather_by_all_to_all(cond_z, "view", Y_GROUPS, YS)
    cond_all = cond_all.reshape(-1, 2 * HS)
    cond_k = cond_all[:, :KPAD]
    cond_vt = cond_all[:, HS:].T
    w_out_all = gather_by_all_to_all(w_out, "head", None, HEADS)

    w_qkv = jnp.concatenate([w_query, w_key, w_value], axis=0)
    q, kv = project((head % 2).astype(jnp.int32).reshape(1), w_qkv, mine, other)

    my_list = lax.dynamic_index_in_dim(neighbours, view, 1, keepdims=False).reshape(-1)
    scalars = jnp.concatenate(
        [my_list, jnp.stack([view.astype(jnp.int32), counts[0], jnp.int32(peers)])]
    )

    plus = minus = kv
    moved = []
    for _ in range(RADIUS):
        plus, minus = shifted(plus, 1), shifted(minus, -1)
        moved.append((plus, minus))
    state = attend_own(q, kv)
    for i, (p, m) in enumerate(moved):
        if i == 2:
            state = attend_cond(q, cond_k, cond_vt, state)
        last = i == RADIUS - 1
        state = attend_near(i + 1, last, scalars, q, p, m, state)
    attended = lax.all_to_all(state, "head", 0, 0, tiled=True)
    return project_out(attended, w_out_all)


def solution(mesh):
    return jax.shard_map(
        per_device,
        mesh=mesh,
        in_specs=(
            P(("view", "head"), None),
            P(),
            P("head", None),
            P("head", None),
            P("head", None),
            P("head", None),
            P("view", None),
            P("head", None),
            P("head", None),
            P(),
            P("view"),
        ),
        out_specs=P(("view", "head"), None),
        check_vma=False,
    )
```
